32 devices in a mesh: parts: 2 (over x), leaf: 16 (over z, y, core).
Axes of the slice: x: 2, y: 2, z: 4, core: 2. Of those that a mesh axis runs over, the one named last changes fastest.
Arguments:
- right_sides: bfloat16 [128, 16384], P('parts', 'leaf'), parts along dimension 0, may hold values from -6 to 6
- near_list: int32 [32, 3], P(('parts', 'leaf')), parts along dimension 0, may hold values from 0 to 15, as said below
- near_blocks: bfloat16 [32, 3, 1024, 1024], P(('parts', 'leaf')), parts along dimension 0, may hold values from -0.02734375 to 0.02734375
- inverse_list: int32 [32, 2], P(('parts', 'leaf')), parts along dimension 0, may hold values from 0 to 15, as said below
- inverse_blocks: bfloat16 [32, 2, 1024, 1024], P(('parts', 'leaf')), parts along dimension 0, may hold values from -0.03125 to 0.03125
- leaf_bases: bfloat16 [32, 1024, 128], P(('parts', 'leaf')), parts along dimension 0, may hold values from -0.1875 to 0.1875
- transfers: bfloat16 [2, 2, 128, 128], replicated, may hold values from -0.375 to 0.375
- couple_list: int32 [32, 3, 4], P(('parts', 'leaf')), parts along dimension 0, may hold values from 0 to 15, as said below
- couple_blocks: bfloat16 [32, 3, 4, 128, 128], P(('parts', 'leaf')), parts along dimension 0, may hold values from -0.125 to 0.125
Outputs:
- solution: float32 [128, 16384], P('parts', 'leaf'), parts along dimension 0
- residual: float32 [128, 16384], P('parts', 'leaf'), parts along dimension 0
The draws below stay inside these ranges and needn't reach their ends.
There are 2 independent parts, one for each index of `parts`. The reference program is written for one: setup_inputs(seed, part) draws one part's arguments, and reference() takes and returns one part's arrays. A program takes and returns all parts, laid end to end along the dimension named above; an argument that names none is the same for every part. Nothing has to cross between parts.
Inputs may be any that keep to these rules, and one draw needn't show every extreme that they name: `near_list`: entry [i, s] lies within 2 of i. `inverse_list`: entry [i, s] lies within 2 of i. `couple_list`: entry [i, l, k] names a cluster of level l, below 16 // 2 ** l.
All inputs are finite; a program needn't handle non-finite values.
Results may differ from the reference program's by a relative error of at most 0.014.
Values may be sent and summed in bfloat16 or wider, within the bound.
No kernel may reach another device: no remote copies, remote signals or barrier semaphores. Data moves between devices by JAX's collectives and lax.ppermute only.
A program may use at most 64 MiB of HBM per device.

```python
import jax
import jax.numpy as jnp
from jax import lax

LEAF = 1024
RANK = 128
RHS = 64
NEAR = 3
SAI = 2
REACH = 2
PARTNERS = 4
LEVELS = 3
LEAVES = 16
ROWS = 16384


def bounded_partners(key, count):
    first_key, second_key = jax.random.split(key)
    offsets = jax.random.randint(first_key, (LEAVES, count), -REACH, REACH + 1)
    center_leaf = jax.random.randint(second_key, (), REACH, LEAVES - REACH)
    row_index = jnp.arange(LEAVES, dtype=jnp.int32)[:, None]
    slot_index = jnp.arange(count, dtype=jnp.int32)[None, :]
    chosen_row = row_index == center_leaf
    offsets = jnp.where(chosen_row & (slot_index == 0), -REACH, offsets)
    offsets = jnp.where(chosen_row & (slot_index == 1), REACH, offsets)
    return jnp.clip(row_index + offsets, 0, LEAVES - 1).astype(jnp.int32)


def draw_near_list(key, part):
    return bounded_partners(jax.random.fold_in(key, 11), NEAR)


def draw_inverse_list(key, part):
    return bounded_partners(jax.random.fold_in(key, 23), SAI)


def draw_couple_list(key, part):
    limits = jnp.array([LEAVES, LEAVES // 2, LEAVES // 4], jnp.int32)[None, :, None]
    drawn = jax.random.randint(jax.random.fold_in(key, 37), (LEAVES, LEVELS, PARTNERS), 0, limits)
    divisors = jnp.array([1, 2, 4], jnp.int32)[None, :]
    row_index = jnp.arange(LEAVES, dtype=jnp.int32)[:, None]
    named = (row_index // divisors + 1) % limits[:, :, 0]
    slot_index = jnp.arange(PARTNERS, dtype=jnp.int32)[None, None, :]
    drawn = jnp.where(slot_index == 0, named[:, :, None], drawn)
    return drawn.astype(jnp.int32)


def levels(key, extent, cuts, smallest, high):
    def one(dim, blocks):
        heights = jax.random.uniform(jax.random.fold_in(jax.random.fold_in(key, 6), dim), (blocks,), jnp.float32, smallest / len(cuts), high / len(cuts))
        return jnp.repeat(jnp.exp(heights), extent[dim] // blocks).reshape((-1,) + (1,) * (len(extent) - dim - 1))

    loudness = one(*cuts[0])
    for cut in cuts[1:]:
        loudness = loudness * one(*cut)
    return loudness


def gaussian(rng, dims, scale, reach, cuts=(), held_as=jnp.bfloat16):
    entries = scale * jax.random.normal(rng, dims, jnp.float32)
    if cuts:
        entries = entries * levels(rng, dims, cuts, -0.22, 0.18)
    return jnp.clip(entries, -reach, reach).astype(held_as)


def setup_inputs(seed: int = 0, part: int = 0) -> dict:
    keys = jax.random.split(jax.random.key(seed), 10)
    own_keys = jax.random.split(jax.random.fold_in(keys[9], part), 10)
    return {
        "right_sides": gaussian(own_keys[0], (RHS, ROWS), 1.0, 6.0, ((1, 16),)),
        "near_list": draw_near_list(jax.random.fold_in(jax.random.fold_in(keys[9], part), 71), part),
        "near_blocks": gaussian(own_keys[2], (LEAVES, NEAR, LEAF, LEAF), (16 * NEAR * LEAF) ** -0.5, 0.02734375, ((0, 16),)),
        "inverse_list": draw_inverse_list(jax.random.fold_in(jax.random.fold_in(keys[9], part), 71), part),
        "inverse_blocks": gaussian(own_keys[4], (LEAVES, SAI, LEAF, LEAF), (16 * SAI * LEAF) ** -0.5, 0.03125, ((0, 16),)),
        "leaf_bases": gaussian(own_keys[5], (LEAVES, LEAF, RANK), LEAF ** -0.5, 0.1875, ((0, 16),)),
        "transfers": gaussian(keys[6], (2, 2, RANK, RANK), (2 * RANK) ** -0.5, 0.375),
        "couple_list": draw_couple_list(jax.random.fold_in(jax.random.fold_in(keys[9], part), 71), part),
        "couple_blocks": gaussian(own_keys[8], (LEAVES, LEVELS, PARTNERS, RANK, RANK), (4 * PARTNERS * RANK) ** -0.5, 0.125, ((0, 16),)),
    }


exact_mode = lax.Precision.HIGHEST


def to_half(values):
    return lax.optimization_barrier(values.astype(jnp.bfloat16))


def leaf_major(vectors):
    return jnp.transpose(vectors.reshape(vectors.shape[0], LEAVES, LEAF), (1, 0, 2))


def apply_blocks(vectors, partner_lists, blocks):
    grouped = leaf_major(vectors)

    def one_leaf(leaf_index):
        running = jnp.zeros(grouped.shape[1:], jnp.float32)
        for slot_index in range(partner_lists.shape[1]):
            partner = partner_lists[leaf_index, slot_index]
            chosen = lax.dynamic_index_in_dim(grouped, partner, 0, keepdims=False)
            running = running + jnp.dot(chosen, blocks[leaf_index, slot_index], preferred_element_type=jnp.float32)
        return running

    outcome = lax.map(one_leaf, jnp.arange(LEAVES, dtype=jnp.int32))
    return jnp.transpose(outcome, (1, 0, 2)).reshape(vectors.shape[0], LEAVES * LEAF)


def lift(coeffs, child_maps):
    grouped = coeffs.reshape(coeffs.shape[0] // 2, 2, coeffs.shape[1], coeffs.shape[2]).astype(jnp.float32)
    left_part = jnp.einsum("prs,st->prt", grouped[:, 0], child_maps[0].astype(jnp.float32), precision=exact_mode)
    right_part = jnp.einsum("prs,st->prt", grouped[:, 1], child_maps[1].astype(jnp.float32), precision=exact_mode)
    return to_half(left_part + right_part)


def descend(coarse, lower_count, child_maps):
    parity = jnp.arange(lower_count, dtype=jnp.int32) % 2
    spread = jnp.repeat(coarse, 2, axis=0)
    chosen = child_maps[parity].astype(jnp.float32)
    return jnp.einsum("prs,pts->prt", spread, chosen, precision=exact_mode)


def far_field(vectors, leaf_bases, transfers, couple_list, couple_blocks):
    grouped = leaf_major(vectors).astype(jnp.float32)
    bases_wide = leaf_bases.astype(jnp.float32)
    coeff_zero = to_half(jnp.einsum("lrj,ljs->lrs", grouped, bases_wide, precision=exact_mode))
    coeff_one = lift(coeff_zero, transfers[0])
    coeff_two = lift(coeff_one, transfers[1])
    fields = []
    for tree_level, coeff_table in enumerate((coeff_zero, coeff_one, coeff_two)):
        chosen = coeff_table[couple_list[:, tree_level]].astype(jnp.float32)
        level_blocks = couple_blocks[:, tree_level].astype(jnp.float32)
        fields.append(jnp.einsum("lkrs,lkst->lrt", chosen, level_blocks, precision=exact_mode))
    pair_one = fields[1][0::2] + fields[1][1::2]
    pair_two = fields[2][0::2] + fields[2][1::2]
    quad_sum = pair_two[0::2] + pair_two[1::2]
    down_one = pair_one + descend(quad_sum, LEAVES // 2, transfers[1])
    leaf_field = fields[0] + descend(down_one, LEAVES, transfers[0])
    rounded = to_half(leaf_field).astype(jnp.float32)
    outcome = jnp.einsum("lrs,ljs->lrj", rounded, bases_wide, precision=exact_mode)
    return jnp.transpose(outcome, (1, 0, 2)).reshape(vectors.shape[0], LEAVES * LEAF)


def reference(right_sides, near_list, near_blocks, inverse_list, inverse_blocks, leaf_bases, transfers, couple_list, couple_blocks):
    def operate(half_vector):
        near_part = apply_blocks(half_vector, near_list, near_blocks)
        far_part = far_field(half_vector, leaf_bases, transfers, couple_list, couple_blocks)
        return half_vector.astype(jnp.float32) + near_part + far_part

    def precondition(half_vector):
        return half_vector.astype(jnp.float32) + apply_blocks(half_vector, inverse_list, inverse_blocks)

    wide_sides = right_sides.astype(jnp.float32)
    iterate_one = precondition(right_sides)
    residual_one = wide_sides - operate(to_half(iterate_one))
    solution = iterate_one + precondition(to_half(residual_one))
    residual = wide_sides - operate(to_half(solution))
    return solution, residual
```

```python
import functools

import jax
import jax.numpy as jnp
from jax import lax
from jax.experimental import pallas as pl
from jax.experimental.pallas import tpu as pltpu
from jax.sharding import PartitionSpec as P

REACH = 2
F32 = jnp.float32
BF16 = jnp.bfloat16
VM = pl.BlockSpec(memory_space=pltpu.VMEM)
SM = pl.BlockSpec(memory_space=pltpu.SMEM)


def swap(value, pairs):
    return lax.ppermute(value, "leaf", pairs)


def xor_pairs(count, mask):
    return [(source, source ^ mask) for source in range(count)]


def odd_edges(count):
    inner = [(source, source + 2 if source & 2 else source - 2) for source in range(2, count - 2)]
    ends = [(0, 1), (1, 0), (count - 2, count - 1), (count - 1, count - 2)]
    return inner + ends


def split_pairs(count, mask):
    return [(source, source ^ mask ^ (2 * (source & 1))) for source in range(count)]


def window_slot(relative, place):
    core, side = place % 2, place // 2 % 2
    left, right = jnp.where(side == 0, 3, 2), jnp.where(side == 0, 2, 3)
    near = jnp.where((relative == 1) == (core == 0), 1, 4)
    far = jnp.where(relative < 0, left, right)
    return jnp.where(relative == 0, 0, jnp.where(abs(relative) == 1, near, far))


def exchange(value, count):
    place = lax.axis_index("leaf")
    core, side = place % 2, place // 2 % 2
    odd = swap(value, odd_edges(count))
    even = swap(value, xor_pairs(count, 2))
    partner = swap(value, xor_pairs(count, 1))
    forward = swap(jnp.where(core == side, even, odd), xor_pairs(count, 1))
    return value, partner, even, odd, forward


def block_sum(place, list_ref, pieces, stack, blocks, slots):
    for index, piece in enumerate(pieces):
        stack[index] = piece[:, : stack.shape[2]]
    total = None
    for slot in range(slots):
        spot = window_slot(list_ref[0, slot] - place, place)
        part = jnp.dot(stack[spot], blocks[slot], preferred_element_type=F32)
        total = part if total is None else total + part
    return total


def smooth_kernel(has_base, place_ref, list_ref, *refs):
    pieces, refs = refs[:5], refs[5:]
    if has_base:
        base, refs = refs[0], refs[1:]
    blocks, bases, wide, half, coeff, stack = refs
    place = place_ref[0]
    total = block_sum(place, list_ref, pieces, stack, blocks, blocks.shape[0])
    total = total + pieces[0][...].astype(F32)
    if has_base:
        total = total + base[...]
    wide[...] = total
    rounded = total.astype(BF16)
    size = rounded.shape[1]
    half[:, :size] = rounded
    coeffs = jnp.dot(rounded, bases[...], preferred_element_type=F32).astype(BF16)
    half[:, size:] = coeffs
    coeff[...] = coeffs


def near_kernel(place_ref, list_ref, *refs):
    pieces, (sides, blocks, out, stack) = refs[:5], refs[5:]
    total = block_sum(place_ref[0], list_ref, pieces, stack, blocks, blocks.shape[0])
    size = stack.shape[2]
    out[...] = sides[...].astype(F32) - pieces[0][:, :size].astype(F32) - total


def far_kernel(offsets, place_ref, *refs):
    tables, (kernel_map, bases, partial, out) = refs[: len(offsets)], refs[len(offsets) :]
    place = place_ref[0]
    core = place % 2
    field = None
    for table, offset in zip(tables, offsets):
        for row in range(table.shape[0]):
            leaf = offset(place, core, row)
            part = jnp.dot(table[row], kernel_map[leaf], preferred_element_type=F32)
            field = part if field is None else field + part
    far = lax.dot_general(
        field.astype(BF16), bases[...], (((1,), (1,)), ((), ())), preferred_element_type=F32
    )
    out[...] = (partial[...] - far).astype(out.dtype)


def far_loop_kernel(place_ref, table, kernel_map, bases, partial, out):
    def step(leaf, field):
        return field + jnp.dot(table[leaf], kernel_map[leaf], preferred_element_type=F32)

    field = lax.fori_loop(0, table.shape[0], step, jnp.zeros(table.shape[1:], F32))
    far = lax.dot_general(
        field.astype(BF16), bases[...], (((1,), (1,)), ((), ())), preferred_element_type=F32
    )
    out[...] = (partial[...] - far).astype(out.dtype)


def scatter_kernel(list_ref, blocks, pair_out, quad_out, pair_sum, quad_sum):
    for level, total, out in ((1, pair_sum, pair_out), (2, quad_sum, quad_out)):
        total[...] = jnp.zeros_like(total)
        for slot in range(blocks.shape[1]):
            cluster = list_ref[0, level, slot]
            total[cluster] += blocks[level, slot].astype(F32)
        out[...] = total[...].astype(out.dtype)


def fold_kernel(place_ref, list_ref, blocks, maps, pair_a, pair_b, quads, out, total):
    place = place_ref[0]
    first, second = place % 2, place // 2 % 2
    total[...] = jnp.zeros_like(total)
    for slot in range(blocks.shape[1]):
        total[list_ref[0, 0, slot]] += blocks[0, slot].astype(F32)

    def turned(left, child_map):
        return lax.dot_general(
            left.astype(BF16), child_map, (((1,), (1,)), ((), ())), preferred_element_type=F32
        )

    def step(quad, carry):
        coarse = sum(ref[quad].astype(F32) for ref in quads)
        coarse = turned(coarse, maps[1, second]).astype(BF16)
        for half in range(2):
            pair = 2 * quad + half
            middle = jnp.dot(maps[1, half], coarse, preferred_element_type=F32)
            middle = middle + pair_a[pair].astype(F32) + pair_b[pair].astype(F32)
            middle = turned(middle, maps[0, first]).astype(BF16)
            for child in range(2):
                leaf = 2 * pair + child
                fine = jnp.dot(maps[0, child], middle, preferred_element_type=F32)
                out[leaf] = (fine + total[leaf]).astype(BF16)
        return carry

    lax.fori_loop(0, out.shape[0] // 4, step, 0)


def shards(
    count,
    right_sides,
    near_list,
    near_blocks,
    inverse_list,
    inverse_blocks,
    leaf_bases,
    transfers,
    couple_list,
    couple_blocks,
):
    rows, size = right_sides.shape
    rank = leaf_bases.shape[2]
    place = lax.axis_index("leaf")
    place_ref = place.astype(jnp.int32).reshape(1)
    near, inverse, bases, couples = near_blocks[0], inverse_blocks[0], leaf_bases[0], couple_blocks[0]
    shape = jax.ShapeDtypeStruct
    one = xor_pairs(count, 1)

    def call(kernel, out_shape, scratch, ints, *operands):
        return pl.pallas_call(
            kernel,
            out_shape=out_shape,
            in_specs=[SM] * ints + [VM] * (len(operands) - ints),
            out_specs=jax.tree.map(lambda _: VM, out_shape),
            scratch_shapes=scratch,
            compiler_params=pltpu.CompilerParams(vmem_limit_bytes=24 << 20),
        )(*operands)

    window = [pltpu.VMEM((5, rows, size), BF16)]

    def smooth(pieces, base):
        extra = () if base is None else (base,)
        return call(
            functools.partial(smooth_kernel, base is not None),
            (shape((rows, size), F32), shape((rows, size + rank), BF16), shape((rows, rank), BF16)),
            window,
            2,
            place_ref,
            inverse_list,
            *pieces,
            *extra,
            inverse,
            bases,
        )

    def gather(coeff, half, even):
        if count != 16:
            return [lax.all_gather(coeff, "leaf", axis=0)], None
        other = swap(coeff, one)
        both = jnp.stack([coeff, other])
        masks = (12, 8, 4)
        got = [swap(both, split_pairs(count, mask)) for mask in masks]
        mine = jnp.concatenate([even[None, :, size:]] + got)
        theirs = swap(mine, one)

        def of_pair(place, core, row):
            return place ^ row

        def of_mine(place, core, row):
            if row == 0:
                return place ^ 2
            return place ^ masks[(row - 1) // 2] ^ (2 * core) ^ ((row - 1) % 2)

        def of_theirs(place, core, row):
            return of_mine(place ^ 1, 1 - core, row)

        return [both, mine, theirs], [of_pair, of_mine, of_theirs]

    def operate(half, coeff, kernel_map, dtype):
        pieces = exchange(half, count)
        tables, offsets = gather(coeff, half, pieces[2])
        partial = call(
            near_kernel,
            shape((rows, size), F32),
            window,
            2,
            place_ref,
            near_list,
            *pieces,
            right_sides,
            near,
        )
        kernel = far_loop_kernel if offsets is None else functools.partial(far_kernel, offsets)
        return call(
            kernel, shape((rows, size), dtype), [], 1, place_ref, *tables, kernel_map, bases, partial
        )

    pieces = exchange(right_sides, count)
    pair_own, quad_own = call(
        scatter_kernel,
        (shape((count // 2, rank, rank), BF16), shape((count // 4, rank, rank), BF16)),
        [pltpu.VMEM((count // 2, rank, rank), F32), pltpu.VMEM((count // 4, rank, rank), F32)],
        1,
        couple_list,
        couples,
    )
    quad_side = swap(quad_own, xor_pairs(count, 2))
    pair_other, quad_other, quad_cross = swap(pair_own, one), swap(quad_own, one), swap(quad_side, one)

    def fold(place_ref, list_ref, blocks, maps, pair_a, pair_b, qa, qb, qc, qd, out, total):
        fold_kernel(place_ref, list_ref, blocks, maps, pair_a, pair_b, (qa, qb, qc, qd), out, total)

    kernel_map = call(
        fold,
        shape((count, rank, rank), BF16),
        [pltpu.VMEM((count, rank, rank), F32)],
        2,
        place_ref,
        couple_list,
        couples,
        transfers,
        pair_own,
        pair_other,
        quad_own,
        quad_side,
        quad_other,
        quad_cross,
    )
    first, first_half, first_coeff = smooth(pieces, None)
    left = operate(first_half, first_coeff, kernel_map, BF16)
    second, second_half, second_coeff = smooth(exchange(left, count), first)
    residual = operate(second_half, second_coeff, kernel_map, F32)
    return second, residual


def solution(mesh):
    return jax.shard_map(
        functools.partial(shards, mesh.shape["leaf"]),
        mesh=mesh,
        in_specs=(
            P("parts", "leaf"),
            P(("parts", "leaf"), None),
            P(("parts", "leaf"), None, None, None),
            P(("parts", "leaf"), None),
            P(("parts", "leaf"), None, None, None),
            P(("parts", "leaf"), None, None),
            P(),
            P(("parts", "leaf"), None, None),
            P(("parts", "leaf"), None, None, None, None),
        ),
        out_specs=(P("parts", "leaf"), P("parts", "leaf")),
        check_vma=False,
    )
```
